256 devices in a mesh: ab: 128 (over z, y, x_hi, core), ij: 2 (over x_lo).
Axes of the slice: x: 4 (x_hi: 2, x_lo: 2; x = x_hi * 2 + x_lo), y: 4, z: 8, core: 2. Of those that a mesh axis runs over, the one named last changes fastest.
Arguments:
- amplitudes: float32 [1024, 2048], P('ab', 'ij'), may hold values from -6 to 6
- integrals: float32 [131072, 2048], P('ab'), may hold values from -0.125 to 0.125
- occ_pairs: float32 [1024], P(('ab', 'ij')), may hold values from -2 to -0.5
- vir_pairs: float32 [131072], P('ab'), may hold values from 1 to 4
Outputs:
- update: float32 [1024, 131072], P(('ab', 'ij'))
The draws below stay inside these ranges and needn't reach their ends.
All inputs are finite; a program needn't handle non-finite values.
Results may differ from the reference program's by a relative error of at most 0.00007.
Values sent between devices are 32-bit elements; how exact they have to be, the bound alone decides.
A program may use at most 64 MiB of HBM per device.

```python
import jax
import jax.numpy as jnp
from jax import lax

CD = 2048
IJ = 1024
AB = 131072


def steps_of(stream_key, shape, shards, smallest, largest):
    def one(position, shards_of):
        draws = jax.random.uniform(jax.random.fold_in(jax.random.fold_in(stream_key, 6), position), (shards_of,), jnp.float32, smallest / len(shards), largest / len(shards))
        return jnp.repeat(jnp.exp(draws), shape[position] // shards_of).reshape((-1,) + (1,) * (len(shape) - position - 1))

    loudness = one(*shards[0])
    for cut in shards[1:]:
        loudness = loudness * one(*cut)
    return loudness


def bell_draw(stream_key, shape, deviation, reach, shards=(), dtype=jnp.bfloat16):
    gain = steps_of(stream_key, shape, shards, -0.22, 0.18) if shards else 1.0
    values = jax.random.normal(stream_key, shape, jnp.float32) * deviation * gain
    return jnp.minimum(jnp.maximum(values, -reach), reach).astype(dtype)


def setup_inputs(seed: int = 0) -> dict:
    splits = jax.random.split(jax.random.key(seed), 5)
    return {
        "amplitudes": bell_draw(splits[0], (IJ, CD), 1.0, 6.0, ((0, 128), (1, 2)), jnp.float32),
        "integrals": bell_draw(splits[1], (AB, CD), CD ** -0.5, 0.125, ((0, 128),), jnp.float32),
        "occ_pairs": jnp.clip(-2.0 + 1.5 * jax.random.uniform(splits[2], (IJ,), jnp.float32) ** steps_of(splits[2], (IJ,), ((0, 256),), -0.2, 0.2), -2.0, -0.5),
        "vir_pairs": jnp.clip(1.0 + 3.0 * jax.random.uniform(splits[3], (AB,), jnp.float32) ** steps_of(splits[3], (AB,), ((0, 128),), -0.2, 0.2), 1.0, 4.0),
    }


def reference(amplitudes, integrals, occ_pairs, vir_pairs):
    residual = jnp.dot(amplitudes, integrals.T, precision=lax.Precision.HIGHEST, preferred_element_type=jnp.float32)
    return residual / (vir_pairs[None, :] - occ_pairs[:, None])
```

```python
import functools

import jax
import jax.numpy as jnp
from jax import lax
from jax.experimental import pallas as pl
from jax.experimental.pallas import tpu as pltpu
from jax.sharding import Mesh
from jax.sharding import PartitionSpec as P

AXES = ("z", "y", "xh", "c", "xl")
MESH = pl.DeviceIdType.MESH
NT = (((1,), (1,)), ((), ()))

DIST = (4, 3, 5, 2, 6, 1, 7, 0)
GROUPS = ((0, 1), (1, 2), (3, 2), (5, 2), (7, 1))
NG = len(GROUPS)
PIECES = 8


def split(x):
    hi = x.astype(jnp.bfloat16)
    lo = (x - hi.astype(jnp.float32)).astype(jnp.bfloat16)
    return hi, lo


def kernel(
    amp_ref, int_ref, occ_ref, vir_ref, out_ref,
    flat, etile, gath, ener, stage, bhi, blo, acat, res,
    b_sem, z_send, z_recv, y_send, y_recv, x_send, x_recv, c_send, c_recv,
    e_send, e_recv, r_send, r_recv, own_sem,
):
    z, y, xh, c, xl = (lax.axis_index(a) for a in AXES)
    block = ((z * 4 + y) * 2 + xh) * 2 + c
    q_me = c * 8 + xh * 4 + y
    partner = (z, y, 1 - xh, c, 1 - xl)
    sibling = (z, y, xh, 1 - c, xl)

    def piece(i):
        rows = pl.ds(i * 128, 128)
        return pltpu.make_async_copy(int_ref.at[rows, :], stage.at[rows, :], b_sem.at[i])

    for i in range(PIECES):
        piece(i).start()

    barrier = pltpu.get_barrier_semaphore()
    peers = [(lax.rem(z + d, 8), y, xh, c, xl) for d in range(1, 8)]
    peers += [(lax.rem(z + d, 8), y, xh, c, 1 - xl) for d in range(8)]
    peers += [(z, lax.rem(y + d, 4), xh, c, xl) for d in range(1, 4)]
    peers += [partner, sibling]
    for peer in peers:
        pl.semaphore_signal(barrier, inc=1, device_id=peer, device_id_type=MESH)

    for s in range(8):
        flat[pl.ds(s, 8, stride=8), :] = amp_ref[:, pl.ds(s * 128, 128)]
    lane_row = lax.broadcasted_iota(jnp.int32, (8, 128), 0)
    energy = jnp.where(lane_row % 4 == 0, occ_ref[0], occ_ref[1])
    energy = jnp.where(lane_row % 4 == 2, occ_ref[2], energy)
    energy = jnp.where(lane_row % 4 == 3, occ_ref[3], energy)
    etile[...] = energy
    ener[7, pl.ds(pl.multiple_of(q_me * 8, 8), 8), :] = energy
    gath[7, xl, pl.ds(pl.multiple_of(q_me * 32, 32), 32), :] = flat[
        pl.ds(pl.multiple_of(xl * 32, 32), 32), :
    ]

    def prepare(i):
        piece(i).wait()

        def body(j, carry):
            rows = pl.ds(pl.multiple_of(i * 128 + j * 16, 16), 16)
            hi, lo = split(stage[rows, :])
            bhi[rows, :] = hi
            blo[rows, :] = lo
            return carry

        lax.fori_loop(0, 8, body, 0)

    prepare(0)
    pl.semaphore_wait(barrier, len(peers))

    def remote(src, dst, send, recv, device):
        return pltpu.make_async_remote_copy(
            src_ref=src, dst_ref=dst, send_sem=send, recv_sem=recv,
            device_id=device, device_id_type=MESH,
        )

    e_rows = pl.ds(pl.multiple_of(q_me * 8, 8), 8)
    a_rows = pl.ds(pl.multiple_of(q_me * 32, 32), 32)
    group_of = [g for g, (first, n) in enumerate(GROUPS) for _ in range(n)]
    for k, d in enumerate(DIST):
        zd = lax.rem(z + 8 - d, 8)
        if d:
            remote(
                etile, ener.at[k, e_rows, :], e_send.at[0], e_recv.at[0], (zd, y, xh, c, xl)
            ).start()
    for k, d in enumerate(DIST):
        zd = lax.rem(z + 8 - d, 8)
        for j in ((xl, 1 - xl) if d else (1 - xl,)):
            remote(
                flat.at[pl.ds(pl.multiple_of(j * 32, 32), 32), :],
                gath.at[k, xl, a_rows, :],
                z_send, z_recv.at[group_of[k]], (zd, y, xh, c, j),
            ).start()

    x_rows = pl.ds(pl.multiple_of((c * 8 + xh * 4) * 32, 128), 128)
    c_rows = pl.ds(pl.multiple_of(c * 256, 256), 256)
    ex_rows = pl.ds(pl.multiple_of((c * 8 + xh * 4) * 8, 32), 32)
    ec_rows = pl.ds(pl.multiple_of(c * 64, 64), 64)

    def slots(g):
        first, n = GROUPS[g]
        return pl.ds(first, n)

    def take(ref, recv):
        remote(ref, ref, own_sem, recv, sibling).wait_recv()

    def z_to_y(g):
        if g == NG - 1:
            take(gath.at[slots(g), 0, pl.ds(0, 32), :], z_recv.at[g])
        else:
            take(gath.at[slots(g), :, pl.ds(0, 32), :], z_recv.at[g])
        if g == 0:
            take(ener.at[0, pl.ds(0, 56), :], e_recv.at[0])
        for d in (2, 1, 3):
            peer = (z, lax.rem(y + d, 4), xh, c, xl)
            mine = gath.at[slots(g), :, a_rows, :]
            remote(mine, mine, y_send, y_recv.at[g], peer).start()
            if g == 0:
                mine = ener.at[:, e_rows, :]
                remote(mine, mine, e_send.at[1], e_recv.at[1], peer).start()

    def y_to_x(g):
        take(gath.at[slots(g), :, pl.ds(0, 96), :], y_recv.at[g])
        mine = gath.at[slots(g), :, x_rows, :]
        remote(mine, mine, x_send, x_recv.at[g], partner).start()
        if g == 0:
            take(ener.at[:, pl.ds(0, 24), :], e_recv.at[1])
            mine = ener.at[:, ex_rows, :]
            remote(mine, mine, e_send.at[2], e_recv.at[2], partner).start()

    def x_to_c(g):
        take(gath.at[slots(g), :, pl.ds(0, 128), :], x_recv.at[g])
        mine = gath.at[slots(g), :, c_rows, :]
        remote(mine, mine, c_send, c_recv.at[g], sibling).start()
        if g == 0:
            take(ener.at[:, pl.ds(0, 32), :], e_recv.at[2])
            mine = ener.at[:, ec_rows, :]
            remote(mine, mine, e_send.at[3], e_recv.at[3], sibling).start()

    upper = lax.broadcasted_iota(jnp.int32, (8, 8, 128), 1) < 4
    home = pl.ds(pl.multiple_of(block * 32, 32), 32)

    def multiply(g):
        first, n = GROUPS[g]
        m = 64 * n
        take(gath.at[slots(g), :, pl.ds(0, 256), :], c_recv.at[g])
        if g == 0:
            take(ener.at[:, pl.ds(0, 64), :], e_recv.at[3])
        for i in range(n):
            for h in range(2):
                for s in range(8):
                    hi, lo = split(gath[first + i, h, pl.ds(s, 64, stride=8), :])
                    cols = pl.ds((h * 8 + s) * 128, 128)
                    acat[pl.ds(64 * i, 64), cols] = hi
                    acat[pl.ds(m + 64 * i, 64), cols] = lo
        occ = []
        for i in range(n):
            pairs = ener[first + i].reshape(8, 2, 8, 128)
            occ.append(jnp.where(upper, pairs[:, 0], pairs[:, 1]))

        for nb in range(4):
            cols = pl.ds(nb * 256, 256)
            high = lax.dot_general(
                acat[pl.ds(0, 2 * m), :], bhi[cols, :], NT, preferred_element_type=jnp.float32
            )
            low = lax.dot_general(
                acat[pl.ds(0, m), :], blo[cols, :], NT, preferred_element_type=jnp.float32
            )
            total = high[:m] + (high[m:] + low)
            for i in range(n):
                tiles = []
                for t in range(2):
                    value = total[64 * i : 64 * i + 64, 128 * t : 128 * t + 128].reshape(8, 8, 128)
                    vir = vir_ref[pl.ds(nb * 2 + t, 1), :]
                    tiles.append(value / (vir[None] - occ[i]))
                even = jnp.where(upper, tiles[0], pltpu.roll(tiles[1], 4, 1))
                odd = jnp.where(upper, pltpu.roll(tiles[0], 4, 1), tiles[1])
                for b in range(8):
                    res[first + i, 2 * b, pl.ds(nb * 8, 8), :] = even[b]
                    res[first + i, 2 * b + 1, pl.ds(nb * 8, 8), :] = odd[b]

        for i in range(n):
            k = first + i
            zd = lax.rem(z + DIST[k], 8)

            def send(step, carry):
                q = lax.rem(q_me + step, 16)
                cd = q // 8
                xd = lax.rem(q // 4, 2)
                target = (zd, lax.rem(q, 4), xd, cd, lax.rem(xl + xd + 2 - xh, 2))
                remote(res.at[k, q], out_ref.at[home, :], r_send, r_recv, target).start()
                return carry

            lax.fori_loop(0 if DIST[k] else 1, 16, send, 0)

    z_to_y(0)
    prepare(1)
    prepare(2)
    z_to_y(1)
    y_to_x(0)
    prepare(3)
    prepare(4)
    prepare(5)
    z_to_y(2)
    y_to_x(1)
    x_to_c(0)
    prepare(6)
    prepare(7)
    z_to_y(3)
    z_to_y(4)
    multiply(0)
    y_to_x(2)
    x_to_c(1)
    y_to_x(3)
    multiply(1)
    x_to_c(2)
    y_to_x(4)
    x_to_c(3)
    multiply(2)
    x_to_c(4)
    multiply(3)
    multiply(4)

    own = pltpu.make_async_copy(res.at[7, q_me], out_ref.at[home, :], own_sem)
    own.start()
    own.wait()

    def sent(ref, send):
        remote(ref, ref, send, own_sem, sibling).wait_send()

    sent(gath.at[pl.ds(0, 7), :, pl.ds(0, 32), :], z_send)
    sent(flat.at[pl.ds(0, 32), :], z_send)
    sent(gath.at[:, :, pl.ds(0, 96), :], y_send)
    sent(gath.at[:, :, pl.ds(0, 128), :], x_send)
    sent(gath.at[:, :, pl.ds(0, 256), :], c_send)
    sent(ener.at[0, pl.ds(0, 56), :], e_send.at[0])
    sent(ener.at[:, pl.ds(0, 24), :], e_send.at[1])
    sent(ener.at[:, pl.ds(0, 32), :], e_send.at[2])
    sent(ener.at[:, pl.ds(0, 64), :], e_send.at[3])
    sent(out_ref.at[pl.ds(0, 127 * 32), :], r_send)
    take(out_ref.at[pl.ds(0, 127 * 32), :], r_recv)


def shards(amplitudes, integrals, occ_pairs, vir_pairs):
    f32, bf16 = jnp.float32, jnp.bfloat16
    dma = pltpu.SemaphoreType.DMA
    out = pl.pallas_call(
        kernel,
        out_shape=jax.ShapeDtypeStruct((4096, 128), f32),
        in_specs=[
            pl.BlockSpec(memory_space=pltpu.VMEM),
            pl.BlockSpec(memory_space=pl.ANY),
            pl.BlockSpec(memory_space=pltpu.SMEM),
            pl.BlockSpec(memory_space=pltpu.VMEM),
        ],
        out_specs=pl.BlockSpec(memory_space=pl.ANY),
        scratch_shapes=[
            pltpu.VMEM((64, 128), f32),
            pltpu.VMEM((8, 128), f32),
            pltpu.VMEM((8, 2, 512, 128), f32),
            pltpu.VMEM((8, 128, 128), f32),
            pltpu.VMEM((1024, 2048), f32),
            pltpu.VMEM((1024, 2048), bf16),
            pltpu.VMEM((1024, 2048), bf16),
            pltpu.VMEM((256, 2048), bf16),
            pltpu.VMEM((8, 16, 32, 128), f32),
            dma((PIECES,)),
            dma, dma((NG,)), dma, dma((NG,)), dma, dma((NG,)), dma, dma((NG,)),
            dma((4,)), dma((4,)), dma, dma, dma,
        ],
        compiler_params=pltpu.CompilerParams(
            collective_id=0, has_side_effects=True, vmem_limit_bytes=48 << 20
        ),
    )(amplitudes, integrals, occ_pairs, vir_pairs.reshape(8, 128))
    return out.reshape(1024, 4, 128).transpose(1, 0, 2).reshape(4, 131072)


def solution(mesh):
    finer = Mesh(mesh.devices.reshape(8, 4, 2, 2, 2), AXES)
    ab = ("z", "y", "xh", "c")
    in_specs = (P(ab, "xl"), P(ab, None), P(AXES), P(ab))
    return jax.shard_map(
        shards, mesh=finer, in_specs=in_specs, out_specs=P(AXES, None), check_vma=False
    )
```

```python
import jax
import jax.numpy as jnp
from jax import lax
from jax.experimental import pallas as pl
from jax.experimental.pallas import tpu as pltpu
from jax.sharding import Mesh
from jax.sharding import PartitionSpec as P

AXES = ("z", "y", "xh", "c", "xl")
MESH = pl.DeviceIdType.MESH

DIST = (1, 7, 2, 6, 3, 5, 4, 0)
PIECES = 8


def column(dy, dx):
    return dy % 4 + 4 * dx


def split(x):
    hi = x.astype(jnp.bfloat16)
    lo = (x - hi.astype(jnp.float32)).astype(jnp.bfloat16)
    return hi, lo


def kernel(
    amp_hbm, int_hbm, occ_hbm, vir_hbm, out_ref,
    amp, occ_ref, vir_ref, flat, etile, gath, ener, stage, bhi, blo, acat, res,
    in_sem, b_sem, z_send, z_recv, f_send, f_recv, c_send, c_recv,
    e_send, ez_recv, ef_recv, ec_recv, r_send, r_recv, own_sem,
):
    z, y, xh, c, xl = (lax.axis_index(a) for a in AXES)
    block = ((z * 4 + y) * 2 + xh) * 2 + c
    partner = (z, y, 1 - xh, c, 1 - xl)
    sibling = (z, y, xh, 1 - c, xl)

    def along_y(d):
        return (z, lax.rem(y + d, 4), xh, c, xl)

    inputs = [
        pltpu.make_async_copy(amp_hbm, amp, in_sem.at[0]),
        pltpu.make_async_copy(occ_hbm, occ_ref, in_sem.at[1]),
        pltpu.make_async_copy(vir_hbm, vir_ref, in_sem.at[2]),
    ]
    for copy in inputs:
        copy.start()

    def piece(i):
        rows = pl.ds(i * 128, 128)
        return pltpu.make_async_copy(int_hbm.at[rows, :], stage.at[rows, :], b_sem.at[i])

    for i in range(PIECES):
        piece(i).start()

    barrier = pltpu.get_barrier_semaphore()
    peers = [(lax.rem(z + d, 8), y, xh, c, xl) for d in range(1, 8)]
    peers += [(lax.rem(z + d, 8), y, xh, c, 1 - xl) for d in range(8)]
    peers += [along_y(d) for d in range(1, 4)]
    peers += [partner, sibling]
    for peer in peers:
        pl.semaphore_signal(barrier, inc=1, device_id=peer, device_id_type=MESH)

    for copy in inputs:
        copy.wait()
    for s in range(8):
        flat[pl.ds(s, 8, stride=8), :] = amp[:, pl.ds(s * 128, 128)]
    lane_row = lax.broadcasted_iota(jnp.int32, (8, 128), 0)
    energy = jnp.where(lane_row % 4 == 0, occ_ref[0], occ_ref[1])
    energy = jnp.where(lane_row % 4 == 2, occ_ref[2], energy)
    energy = jnp.where(lane_row % 4 == 3, occ_ref[3], energy)
    etile[...] = energy
    ener[0, 0, pl.ds(56, 8), :] = energy
    gath[0, 0, xl, pl.ds(224, 32), :] = flat[pl.ds(pl.multiple_of(xl * 32, 32), 32), :]

    def prepare(i):
        piece(i).wait()

        rows = pl.ds(i * 128, 128)
        hi, lo = split(stage[rows, :].T)
        bhi[:, rows] = hi
        blo[:, rows] = lo

    pl.semaphore_wait(barrier, len(peers))

    def remote(src, dst, send, recv, device):
        return pltpu.make_async_remote_copy(
            src_ref=src, dst_ref=dst, send_sem=send, recv_sem=recv,
            device_id=device, device_id_type=MESH,
        )

    def take(ref, recv):
        remote(ref, ref, own_sem, recv, sibling).wait_recv()

    for k, d in enumerate(DIST):
        zd = lax.rem(z + 8 - d, 8)
        rows = pl.ds(k * 32, 32)
        for j in (xl, 1 - xl) if d else (1 - xl,):
            remote(
                flat.at[pl.ds(pl.multiple_of(j * 32, 32), 32), :],
                gath.at[0, 0, xl, rows, :],
                z_send, z_recv.at[k // 4], (zd, y, xh, c, j),
            ).start()
        if d:
            remote(
                etile, ener.at[0, 0, pl.ds(k * 8, 8), :], e_send, ez_recv.at[k // 4],
                (zd, y, xh, c, xl),
            ).start()

    def part(col, core, run):
        return gath.at[col, core, :, pl.ds(run * 128, 128), :]

    def levels(col, core, run):
        return ener.at[col, core, pl.ds(run * 32, 32), :]

    def forward(col, run, to, device):
        remote(
            part(col, 0, run), part(to, 0, run), f_send, f_recv.at[to, run], device
        ).start()
        remote(
            levels(col, 0, run), levels(to, 0, run), e_send, ef_recv.at[to, run], device
        ).start()

    def arrived(col, run):
        take(part(col, 0, run), f_recv.at[col, run])
        take(levels(col, 0, run), ef_recv.at[col, run])

    def exchange(col, run):
        remote(part(col, 0, run), part(col, 1, run), c_send, c_recv.at[col, run], sibling).start()
        remote(
            levels(col, 0, run), levels(col, 1, run), e_send, ec_recv.at[col, run], sibling
        ).start()

    upper = lax.broadcasted_iota(jnp.int32, (2, 8, 128), 1) < 4
    home = pl.ds(pl.multiple_of(block * 32, 32), 32)

    def multiply(parts):
        m = 32 * len(parts)
        occ = []
        for i, (col, run) in enumerate(parts):
            take(part(col, 1, run), c_recv.at[col, run])
            take(levels(col, 1, run), ec_recv.at[col, run])
            for core in range(2):
                base = 32 * i + 16 * core
                for h in range(2):
                    for s in range(8):
                        rows = pl.ds(run * 128 + s, 16, stride=8)
                        hi, lo = split(gath[col, core, h, rows, :])
                        lanes = pl.ds((h * 8 + s) * 128, 128)
                        acat[pl.ds(base, 16), lanes] = hi
                        acat[pl.ds(m + base, 16), lanes] = lo
                pairs = ener[col, core, pl.ds(run * 32, 32), :].reshape(2, 2, 8, 128)
                occ.append(jnp.where(upper, pairs[:, 0], pairs[:, 1]))

        for nb in range(4):
            lanes = pl.ds(nb * 256, 256)
            high = jnp.dot(
                acat[pl.ds(0, 2 * m), :], bhi[:, lanes], preferred_element_type=jnp.float32
            )
            low = jnp.dot(
                acat[pl.ds(0, m), :], blo[:, lanes], preferred_element_type=jnp.float32
            )
            total = high[:m] + (high[m:] + low)
            for i, (col, run) in enumerate(parts):
                for core in range(2):
                    base = 32 * i + 16 * core
                    tiles = []
                    for t in range(2):
                        value = total[base : base + 16, 128 * t : 128 * t + 128]
                        vir = vir_ref[pl.ds(nb * 2 + t, 1), :]
                        tiles.append(
                            value.reshape(2, 8, 128) / (vir[None] - occ[2 * i + core])
                        )
                    even = jnp.where(upper, tiles[0], pltpu.roll(tiles[1], 4, 1))
                    odd = jnp.where(upper, pltpu.roll(tiles[0], 4, 1), tiles[1])
                    for b in range(2):
                        k = 4 * run + 2 * b
                        res[col, core, k, pl.ds(nb * 8, 8), :] = even[b]
                        res[col, core, k + 1, pl.ds(nb * 8, 8), :] = odd[b]

    def give(col, slots):
        yd = lax.rem(y + col % 4, 4)
        xhd, xld = (1 - xh, 1 - xl) if col >= 4 else (xh, xl)
        for k in slots:
            zd = lax.rem(z + DIST[k], 8)
            for core in range(2):
                if col == 0 and core == 0 and DIST[k] == 0:
                    continue
                cd = 1 - c if core else c
                remote(
                    res.at[col, core, k], out_ref.at[home, :], r_send, r_recv,
                    (zd, yd, xhd, cd, xld),
                ).start()

    here, up, far, down = (column(d, 0) for d in range(4))
    over, up_over, far_over, down_over = (column(d, 1) for d in range(4))
    near_slots, far_slots = (2, 3, 0, 1), (6, 4, 5, 7)
    all_slots = (6, 4, 5, 2, 3, 0, 1, 7)

    prepare(0)
    prepare(1)
    prepare(2)
    for run in range(2):
        take(gath.at[0, 0, :, pl.ds(0, 112 if run else 128), :], z_recv.at[run])
        take(ener.at[0, 0, pl.ds(0, 24 if run else 32), :], ez_recv.at[run])
        exchange(here, run)
        forward(here, run, over, partner)
        forward(here, run, down, along_y(1))
        forward(here, run, up, along_y(3))
        if run == 0:
            for i in range(3, 8):
                prepare(i)
        multiply([(here, run)])
        give(here, (6, 4, 5, 7) if run else (2, 3, 0, 1))
    for run in range(2):
        arrived(over, run)
        exchange(over, run)
        for col in (up, down):
            arrived(col, run)
            exchange(col, run)
        if run == 0:
            forward(down, 0, far, along_y(1))
        else:
            forward(up, 1, far, along_y(3))
        forward(over, run, down_over, along_y(1))
        forward(over, run, up_over, along_y(3))
        multiply([(over, run)])
        give(over, (6, 4, 5, 7) if run else (2, 3, 0, 1))
    for run in range(2):
        arrived(far, run)
        exchange(far, run)
        forward(far, run, far_over, partner)
    multiply([(far, 0), (far, 1)])
    give(far, all_slots)
    for run in range(2):
        for col in (up_over, down_over):
            arrived(col, run)
            exchange(col, run)
    multiply([(up_over, 0), (up_over, 1), (down_over, 0), (down_over, 1)])
    give(up_over, all_slots)
    give(down_over, all_slots)
    for run in range(2):
        arrived(far_over, run)
        exchange(far_over, run)
    multiply([(far_over, 0), (far_over, 1)])
    give(far_over, all_slots)
    multiply([(up, 0), (up, 1), (down, 0), (down, 1)])
    give(up, all_slots)
    give(down, all_slots)

    own = pltpu.make_async_copy(res.at[0, 0, 7], out_ref.at[home, :], own_sem)
    own.start()
    own.wait()

    def sent(ref, send):
        remote(ref, ref, send, own_sem, sibling).wait_send()

    sent(gath.at[0, 0, :, pl.ds(0, 240), :], z_send)
    sent(gath.at[pl.ds(0, 7), 0], f_send)
    sent(gath.at[:, 0], c_send)
    sent(ener.at[0, 0, pl.ds(0, 56), :], e_send)
    sent(ener.at[pl.ds(0, 7), 0], e_send)
    sent(ener.at[:, 0], e_send)
    sent(out_ref.at[pl.ds(0, 127 * 32), :], r_send)
    take(out_ref.at[pl.ds(0, 127 * 32), :], r_recv)


def shards(amplitudes, integrals, occ_pairs, vir_pairs):
    f32, bf16 = jnp.float32, jnp.bfloat16
    dma = pltpu.SemaphoreType.DMA
    out = pl.pallas_call(
        kernel,
        out_shape=jax.ShapeDtypeStruct((4096, 128), f32),
        in_specs=[pl.BlockSpec(memory_space=pltpu.HBM)] * 4,
        out_specs=pl.BlockSpec(memory_space=pl.ANY),
        scratch_shapes=[
            pltpu.VMEM((8, 1024), f32),
            pltpu.SMEM((4,), f32),
            pltpu.VMEM((8, 128), f32),
            pltpu.VMEM((64, 128), f32),
            pltpu.VMEM((8, 128), f32),
            pltpu.VMEM((8, 2, 2, 256, 128), f32),
            pltpu.VMEM((8, 2, 64, 128), f32),
            pltpu.VMEM((1024, 2048), f32),
            pltpu.VMEM((2048, 1024), bf16),
            pltpu.VMEM((2048, 1024), bf16),
            pltpu.VMEM((256, 2048), bf16),
            pltpu.VMEM((8, 2, 8, 32, 128), f32),
            dma((3,)), dma((PIECES,)),
            dma, dma((2,)), dma, dma((8, 2)), dma, dma((8, 2)),
            dma, dma((2,)), dma((8, 2)), dma((8, 2)), dma, dma, dma,
        ],
        compiler_params=pltpu.CompilerParams(
            collective_id=0, has_side_effects=True, vmem_limit_bytes=56 << 20
        ),
    )(amplitudes, integrals, occ_pairs, vir_pairs.reshape(8, 128))
    return out.reshape(1024, 4, 128).transpose(1, 0, 2).reshape(4, 131072)


def solution(mesh):
    finer = Mesh(mesh.devices.reshape(8, 4, 2, 2, 2), AXES)
    ab = ("z", "y", "xh", "c")
    in_specs = (P(ab, "xl"), P(ab, None), P(AXES), P(ab))
    return jax.shard_map(
        shards, mesh=finer, in_specs=in_specs, out_specs=P(AXES, None), check_vma=False
    )
```

```python
import jax
import jax.numpy as jnp
from jax import lax
from jax.experimental import pallas as pl
from jax.experimental.pallas import tpu as pltpu
from jax.sharding import Mesh
from jax.sharding import PartitionSpec as P

AXES = ("z", "y", "xh", "c", "xl")
MESH = pl.DeviceIdType.MESH

DIST = (1, 7, 2, 6, 3, 5, 4, 0)
PIECES = 8


def column(dy, dx):
    return dy % 4 + 4 * dx


def split(x):
    hi = x.astype(jnp.bfloat16)
    lo = (x - hi.astype(jnp.float32)).astype(jnp.bfloat16)
    return hi, lo


def kernel(
    amp_hbm, int_hbm, occ_hbm, vir_hbm, out_ref,
    amp, occ_ref, vir_ref, flat, etile, gath, ener, stage, bhi, blo, acat, res,
    in_sem, b_sem, z_send, z_recv, f_send, f_recv, c_send, c_recv,
    e_send, ez_recv, ef_recv, ec_recv, r_send, r_recv, own_sem,
):
    z, y, xh, c, xl = (lax.axis_index(a) for a in AXES)
    block = ((z * 4 + y) * 2 + xh) * 2 + c
    partner = (z, y, 1 - xh, c, 1 - xl)
    sibling = (z, y, xh, 1 - c, xl)

    def along_y(d):
        return (z, lax.rem(y + d, 4), xh, c, xl)

    inputs = [
        pltpu.make_async_copy(amp_hbm, amp, in_sem.at[0]),
        pltpu.make_async_copy(occ_hbm, occ_ref, in_sem.at[1]),
        pltpu.make_async_copy(vir_hbm, vir_ref, in_sem.at[2]),
    ]
    for copy in inputs:
        copy.start()

    def piece(i):
        rows = pl.ds(i * 128, 128)
        return pltpu.make_async_copy(int_hbm.at[rows, :], stage.at[rows, :], b_sem.at[i])

    for i in range(PIECES):
        piece(i).start()

    barrier = pltpu.get_barrier_semaphore()
    peers = [(lax.rem(z + d, 8), y, xh, c, xl) for d in range(1, 8)]
    peers += [(lax.rem(z + d, 8), y, xh, c, 1 - xl) for d in range(8)]
    peers += [along_y(d) for d in range(1, 4)]
    peers += [partner, sibling]
    for peer in peers:
        pl.semaphore_signal(barrier, inc=1, device_id=peer, device_id_type=MESH)

    for copy in inputs:
        copy.wait()
    for s in range(8):
        flat[pl.ds(s, 8, stride=8), :] = amp[:, pl.ds(s * 128, 128)]
    lane_row = lax.broadcasted_iota(jnp.int32, (8, 128), 0)
    energy = jnp.where(lane_row % 4 == 0, occ_ref[0], occ_ref[1])
    energy = jnp.where(lane_row % 4 == 2, occ_ref[2], energy)
    energy = jnp.where(lane_row % 4 == 3, occ_ref[3], energy)
    etile[...] = energy
    ener[0, 0, pl.ds(56, 8), :] = energy
    gath[0, 0, xl, pl.ds(224, 32), :] = flat[pl.ds(pl.multiple_of(xl * 32, 32), 32), :]

    def prepare(i):
        piece(i).wait()

        rows = pl.ds(i * 128, 128)
        hi, lo = split(stage[rows, :].T)
        bhi[:, rows] = hi
        blo[:, rows] = lo

    pl.semaphore_wait(barrier, len(peers))

    def remote(src, dst, send, recv, device):
        return pltpu.make_async_remote_copy(
            src_ref=src, dst_ref=dst, send_sem=send, recv_sem=recv,
            device_id=device, device_id_type=MESH,
        )

    def take(ref, recv):
        remote(ref, ref, own_sem, recv, sibling).wait_recv()

    for k, d in enumerate(DIST):
        zd = lax.rem(z + 8 - d, 8)
        rows = pl.ds(k * 32, 32)
        for j in (xl, 1 - xl) if d else (1 - xl,):
            remote(
                flat.at[pl.ds(pl.multiple_of(j * 32, 32), 32), :],
                gath.at[0, 0, xl, rows, :],
                z_send, z_recv.at[k // 4], (zd, y, xh, c, j),
            ).start()
        if d:
            remote(
                etile, ener.at[0, 0, pl.ds(k * 8, 8), :], e_send, ez_recv.at[k // 4],
                (zd, y, xh, c, xl),
            ).start()

    def part(col, core, run):
        return gath.at[col, core, :, pl.ds(run * 128, 128), :]

    def levels(col, core, run):
        return ener.at[col, core, pl.ds(run * 32, 32), :]

    def forward(col, run, to, device):
        remote(
            part(col, 0, run), part(to, 0, run), f_send, f_recv.at[to, run], device
        ).start()
        remote(
            levels(col, 0, run), levels(to, 0, run), e_send, ef_recv.at[to, run], device
        ).start()

    def arrived(col, run):
        take(part(col, 0, run), f_recv.at[col, run])
        take(levels(col, 0, run), ef_recv.at[col, run])

    def exchange(col, run):
        remote(part(col, 0, run), part(col, 1, run), c_send, c_recv.at[col, run], sibling).start()
        remote(
            levels(col, 0, run), levels(col, 1, run), e_send, ec_recv.at[col, run], sibling
        ).start()

    upper = lax.broadcasted_iota(jnp.int32, (2, 8, 128), 1) < 4
    home = pl.ds(pl.multiple_of(block * 32, 32), 32)

    def multiply(parts):
        m = 32 * len(parts)
        occ = []
        for i, (col, run) in enumerate(parts):
            take(part(col, 1, run), c_recv.at[col, run])
            take(levels(col, 1, run), ec_recv.at[col, run])
            for core in range(2):
                base = 32 * i + 16 * core
                for h in range(2):
                    for s in range(8):
                        rows = pl.ds(run * 128 + s, 16, stride=8)
                        hi, lo = split(gath[col, core, h, rows, :])
                        lanes = pl.ds((h * 8 + s) * 128, 128)
                        acat[pl.ds(base, 16), lanes] = hi
                        acat[pl.ds(m + base, 16), lanes] = lo
                pairs = ener[col, core, pl.ds(run * 32, 32), :].reshape(2, 2, 8, 128)
                occ.append(jnp.where(upper, pairs[:, 0], pairs[:, 1]))

        for nb in range(4):
            lanes = pl.ds(nb * 256, 256)
            high = jnp.dot(
                acat[pl.ds(0, 2 * m), :], bhi[:, lanes], preferred_element_type=jnp.float32
            )
            low = jnp.dot(
                acat[pl.ds(0, m), :], blo[:, lanes], preferred_element_type=jnp.float32
            )
            total = high[:m] + (high[m:] + low)
            for i, (col, run) in enumerate(parts):
                for core in range(2):
                    base = 32 * i + 16 * core
                    tiles = []
                    for t in range(2):
                        value = total[base : base + 16, 128 * t : 128 * t + 128]
                        vir = vir_ref[pl.ds(nb * 2 + t, 1), :]
                        tiles.append(
                            value.reshape(2, 8, 128) / (vir[None] - occ[2 * i + core])
                        )
                    even = jnp.where(upper, tiles[0], pltpu.roll(tiles[1], 4, 1))
                    odd = jnp.where(upper, pltpu.roll(tiles[0], 4, 1), tiles[1])
                    for b in range(2):
                        k = 4 * run + 2 * b
                        res[col, core, k, pl.ds(nb * 8, 8), :] = even[b]
                        res[col, core, k + 1, pl.ds(nb * 8, 8), :] = odd[b]

    def give(col, slots):
        yd = lax.rem(y + col % 4, 4)
        xhd, xld = (1 - xh, 1 - xl) if col >= 4 else (xh, xl)
        for k in slots:
            zd = lax.rem(z + DIST[k], 8)
            for core in range(2):
                if col == 0 and core == 0 and DIST[k] == 0:
                    continue
                cd = 1 - c if core else c
                remote(
                    res.at[col, core, k], out_ref.at[home, :], r_send, r_recv,
                    (zd, yd, xhd, cd, xld),
                ).start()

    here, up, far, down = (column(d, 0) for d in range(4))
    over, up_over, far_over, down_over = (column(d, 1) for d in range(4))
    near_slots, far_slots = (2, 3, 0, 1), (6, 4, 5, 7)
    all_slots = (6, 4, 5, 2, 3, 0, 1, 7)

    for i in range(6):
        prepare(i)
    for run in range(2):
        take(gath.at[0, 0, :, pl.ds(0, 112 if run else 128), :], z_recv.at[run])
        take(ener.at[0, 0, pl.ds(0, 24 if run else 32), :], ez_recv.at[run])
        exchange(here, run)
        forward(here, run, over, partner)
        forward(here, run, down, along_y(1))
        forward(here, run, up, along_y(3))
        if run == 0:
            for i in range(6, 8):
                prepare(i)
        multiply([(here, run)])
        give(here, (6, 4, 5, 7) if run else (2, 3, 0, 1))
    for run in range(2):
        arrived(over, run)
        exchange(over, run)
        for col in (up, down):
            arrived(col, run)
            exchange(col, run)
        if run == 0:
            forward(down, 0, far, along_y(1))
        else:
            forward(up, 1, far, along_y(3))
        forward(over, run, down_over, along_y(1))
        forward(over, run, up_over, along_y(3))
        multiply([(over, run)])
        give(over, (6, 4, 5, 7) if run else (2, 3, 0, 1))
    for run in range(2):
        arrived(far, run)
        exchange(far, run)
        forward(far, run, far_over, partner)
    multiply([(far, 0), (far, 1)])
    give(far, all_slots)
    for run in range(2):
        for col in (up_over, down_over):
            arrived(col, run)
            exchange(col, run)
    multiply([(up_over, 0), (up_over, 1), (down_over, 0), (down_over, 1)])
    give(up_over, all_slots)
    give(down_over, all_slots)
    for run in range(2):
        arrived(far_over, run)
        exchange(far_over, run)
    multiply([(far_over, 0), (far_over, 1)])
    give(far_over, all_slots)
    multiply([(up, 0), (up, 1), (down, 0), (down, 1)])
    give(up, all_slots)
    give(down, all_slots)

    own = pltpu.make_async_copy(res.at[0, 0, 7], out_ref.at[home, :], own_sem)
    own.start()
    own.wait()

    def sent(ref, send):
        remote(ref, ref, send, own_sem, sibling).wait_send()

    sent(gath.at[0, 0, :, pl.ds(0, 240), :], z_send)
    sent(gath.at[pl.ds(0, 7), 0], f_send)
    sent(gath.at[:, 0], c_send)
    sent(ener.at[0, 0, pl.ds(0, 56), :], e_send)
    sent(ener.at[pl.ds(0, 7), 0], e_send)
    sent(ener.at[:, 0], e_send)
    sent(out_ref.at[pl.ds(0, 127 * 32), :], r_send)
    take(out_ref.at[pl.ds(0, 127 * 32), :], r_recv)


def shards(amplitudes, integrals, occ_pairs, vir_pairs):
    f32, bf16 = jnp.float32, jnp.bfloat16
    dma = pltpu.SemaphoreType.DMA
    out = pl.pallas_call(
        kernel,
        out_shape=pltpu.VMEM((4096, 128), f32),
        in_specs=[pl.BlockSpec(memory_space=pltpu.HBM)] * 4,
        out_specs=pl.BlockSpec(memory_space=pl.ANY),
        scratch_shapes=[
            pltpu.VMEM((8, 1024), f32),
            pltpu.SMEM((4,), f32),
            pltpu.VMEM((8, 128), f32),
            pltpu.VMEM((64, 128), f32),
            pltpu.VMEM((8, 128), f32),
            pltpu.VMEM((8, 2, 2, 256, 128), f32),
            pltpu.VMEM((8, 2, 64, 128), f32),
            pltpu.VMEM((1024, 2048), f32),
            pltpu.VMEM((2048, 1024), bf16),
            pltpu.VMEM((2048, 1024), bf16),
            pltpu.VMEM((256, 2048), bf16),
            pltpu.VMEM((8, 2, 8, 32, 128), f32),
            dma((3,)), dma((PIECES,)),
            dma, dma((2,)), dma, dma((8, 2)), dma, dma((8, 2)),
            dma, dma((2,)), dma((8, 2)), dma((8, 2)), dma, dma, dma,
        ],
        compiler_params=pltpu.CompilerParams(
            collective_id=0, has_side_effects=True, vmem_limit_bytes=56 << 20
        ),
    )(amplitudes, integrals, occ_pairs, vir_pairs.reshape(8, 128))
    return out.reshape(1024, 4, 128).transpose(1, 0, 2).reshape(4, 131072)


def solution(mesh):
    finer = Mesh(mesh.devices.reshape(8, 4, 2, 2, 2), AXES)
    ab = ("z", "y", "xh", "c")
    in_specs = (P(ab, "xl"), P(ab, None), P(AXES), P(ab))
    return jax.shard_map(
        shards, mesh=finer, in_specs=in_specs, out_specs=P(AXES, None), check_vma=False
    )
```

```python
import jax
import jax.numpy as jnp
from jax import lax
from jax.experimental import pallas as pl
from jax.experimental.pallas import tpu as pltpu
from jax.sharding import Mesh
from jax.sharding import PartitionSpec as P

AXES = ("z", "y", "xh", "c", "xl")
MESH = pl.DeviceIdType.MESH

DIST = (1, 7, 2, 6, 3, 5, 4, 0)
PIECES = 8


def column(dy, dx):
    return dy % 4 + 4 * dx


def split(x):
    hi = x.astype(jnp.bfloat16)
    lo = (x - hi.astype(jnp.float32)).astype(jnp.bfloat16)
    return hi, lo


def kernel(
    amp_hbm, int_hbm, occ_hbm, vir_hbm, out_ref,
    amp, occ_ref, vir_ref, flat, etile, gath, ener, stage, bhi, blo, acat, res,
    in_sem, b_sem, z_send, z_recv, f_send, f_recv, c_send, c_recv,
    e_send, ez_recv, ef_recv, ec_recv, r_send, r_recv, own_sem,
):
    z, y, xh, c, xl = (lax.axis_index(a) for a in AXES)
    block = ((z * 4 + y) * 2 + xh) * 2 + c
    partner = (z, y, 1 - xh, c, 1 - xl)
    sibling = (z, y, xh, 1 - c, xl)

    def along_y(d):
        return (z, lax.rem(y + d, 4), xh, c, xl)

    inputs = [
        pltpu.make_async_copy(amp_hbm, amp, in_sem.at[0]),
        pltpu.make_async_copy(occ_hbm, occ_ref, in_sem.at[1]),
        pltpu.make_async_copy(vir_hbm, vir_ref, in_sem.at[2]),
    ]
    for copy in inputs:
        copy.start()

    def piece(i):
        rows = pl.ds(i * 128, 128)
        return pltpu.make_async_copy(int_hbm.at[rows, :], stage.at[rows, :], b_sem.at[i])

    for i in range(PIECES):
        piece(i).start()

    barrier = pltpu.get_barrier_semaphore()
    peers = [(lax.rem(z + d, 8), y, xh, c, xl) for d in range(1, 8)]
    peers += [(lax.rem(z + d, 8), y, xh, c, 1 - xl) for d in range(8)]
    peers += [along_y(d) for d in range(1, 4)]
    peers += [partner, sibling]
    for peer in peers:
        pl.semaphore_signal(barrier, inc=1, device_id=peer, device_id_type=MESH)

    for copy in inputs:
        copy.wait()
    for s in range(8):
        flat[pl.ds(s, 8, stride=8), :] = amp[:, pl.ds(s * 128, 128)]
    lane_row = lax.broadcasted_iota(jnp.int32, (8, 128), 0)
    energy = jnp.where(lane_row % 4 == 0, occ_ref[0], occ_ref[1])
    energy = jnp.where(lane_row % 4 == 2, occ_ref[2], energy)
    energy = jnp.where(lane_row % 4 == 3, occ_ref[3], energy)
    etile[...] = energy
    ener[0, 0, pl.ds(56, 8), :] = energy
    gath[0, 0, xl, pl.ds(224, 32), :] = flat[pl.ds(pl.multiple_of(xl * 32, 32), 32), :]

    def prepare(i):
        piece(i).wait()

        rows = pl.ds(i * 128, 128)
        hi, lo = split(stage[rows, :].T)
        bhi[:, rows] = hi
        blo[:, rows] = lo

    pl.semaphore_wait(barrier, len(peers))

    def remote(src, dst, send, recv, device):
        return pltpu.make_async_remote_copy(
            src_ref=src, dst_ref=dst, send_sem=send, recv_sem=recv,
            device_id=device, device_id_type=MESH,
        )

    def take(ref, recv):
        remote(ref, ref, own_sem, recv, sibling).wait_recv()

    for k, d in enumerate(DIST):
        zd = lax.rem(z + 8 - d, 8)
        rows = pl.ds(k * 32, 32)
        for j in (xl, 1 - xl) if d else (1 - xl,):
            remote(
                flat.at[pl.ds(pl.multiple_of(j * 32, 32), 32), :],
                gath.at[0, 0, xl, rows, :],
                z_send, z_recv.at[k // 4], (zd, y, xh, c, j),
            ).start()
        if d:
            remote(
                etile, ener.at[0, 0, pl.ds(k * 8, 8), :], e_send, ez_recv.at[k // 4],
                (zd, y, xh, c, xl),
            ).start()

    def part(col, core, run):
        return gath.at[col, core, :, pl.ds(run * 128, 128), :]

    def levels(col, core, run):
        return ener.at[col, core, pl.ds(run * 32, 32), :]

    def forward(col, run, to, device):
        remote(
            part(col, 0, run), part(to, 0, run), f_send, f_recv.at[to, run], device
        ).start()
        remote(
            levels(col, 0, run), levels(to, 0, run), e_send, ef_recv.at[to, run], device
        ).start()

    def arrived(col, run):
        take(part(col, 0, run), f_recv.at[col, run])
        take(levels(col, 0, run), ef_recv.at[col, run])

    def exchange(col, run):
        remote(part(col, 0, run), part(col, 1, run), c_send, c_recv.at[col, run], sibling).start()
        remote(
            levels(col, 0, run), levels(col, 1, run), e_send, ec_recv.at[col, run], sibling
        ).start()

    upper = lax.broadcasted_iota(jnp.int32, (2, 8, 128), 1) < 4
    home = pl.ds(pl.multiple_of(block * 32, 32), 32)

    def multiply(parts):
        m = 32 * len(parts)
        occ = []
        for i, (col, run) in enumerate(parts):
            take(part(col, 1, run), c_recv.at[col, run])
            take(levels(col, 1, run), ec_recv.at[col, run])
            for core in range(2):
                base = 32 * i + 16 * core
                for h in range(2):
                    for s in range(8):
                        rows = pl.ds(run * 128 + s, 16, stride=8)
                        hi, lo = split(gath[col, core, h, rows, :])
                        lanes = pl.ds((h * 8 + s) * 128, 128)
                        acat[pl.ds(base, 16), lanes] = hi
                        acat[pl.ds(m + base, 16), lanes] = lo
                pairs = ener[col, core, pl.ds(run * 32, 32), :].reshape(2, 2, 8, 128)
                occ.append(jnp.where(upper, pairs[:, 0], pairs[:, 1]))

        for nb in range(4):
            lanes = pl.ds(nb * 256, 256)
            high = jnp.dot(
                acat[pl.ds(0, 2 * m), :], bhi[:, lanes], preferred_element_type=jnp.float32
            )
            low = jnp.dot(
                acat[pl.ds(0, m), :], blo[:, lanes], preferred_element_type=jnp.float32
            )
            total = high[:m] + (high[m:] + low)
            for i, (col, run) in enumerate(parts):
                for core in range(2):
                    base = 32 * i + 16 * core
                    tiles = []
                    for t in range(2):
                        value = total[base : base + 16, 128 * t : 128 * t + 128]
                        vir = vir_ref[pl.ds(nb * 2 + t, 1), :]
                        tiles.append(
                            value.reshape(2, 8, 128) / (vir[None] - occ[2 * i + core])
                        )
                    even = jnp.where(upper, tiles[0], pltpu.roll(tiles[1], 4, 1))
                    odd = jnp.where(upper, pltpu.roll(tiles[0], 4, 1), tiles[1])
                    for b in range(2):
                        k = 4 * run + 2 * b
                        res[col, core, k, pl.ds(nb * 8, 8), :] = even[b]
                        res[col, core, k + 1, pl.ds(nb * 8, 8), :] = odd[b]

    def give(col, slots):
        yd = lax.rem(y + col % 4, 4)
        xhd, xld = (1 - xh, 1 - xl) if col >= 4 else (xh, xl)
        for k in slots:
            zd = lax.rem(z + DIST[k], 8)
            for core in range(2):
                if col == 0 and core == 0 and DIST[k] == 0:
                    continue
                cd = 1 - c if core else c
                remote(
                    res.at[col, core, k], out_ref.at[home, :], r_send, r_recv,
                    (zd, yd, xhd, cd, xld),
                ).start()

    here, up, far, down = (column(d, 0) for d in range(4))
    over, up_over, far_over, down_over = (column(d, 1) for d in range(4))
    near_slots, far_slots = (2, 3, 0, 1), (6, 4, 5, 7)
    all_slots = (6, 4, 5, 2, 3, 0, 1, 7)

    for i in range(6):
        prepare(i)
    for run in range(2):
        take(gath.at[0, 0, :, pl.ds(0, 112 if run else 128), :], z_recv.at[run])
        take(ener.at[0, 0, pl.ds(0, 24 if run else 32), :], ez_recv.at[run])
        exchange(here, run)
        forward(here, run, over, partner)
        forward(here, run, down, along_y(1))
        forward(here, run, up, along_y(3))
        if run == 0:
            for i in range(6, 8):
                prepare(i)
        multiply([(here, run)])
        give(here, (6, 4, 5, 7) if run else (2, 3, 0, 1))
    for run in range(2):
        arrived(over, run)
        exchange(over, run)
        for col in (up, down):
            arrived(col, run)
            exchange(col, run)
        if run == 0:
            forward(down, 0, far, along_y(1))
        else:
            forward(up, 1, far, along_y(3))
        forward(over, run, down_over, along_y(1))
        forward(over, run, up_over, along_y(3))
        multiply([(over, run)])
        give(over, (6, 4, 5, 7) if run else (2, 3, 0, 1))
    for run in range(2):
        arrived(far, run)
        exchange(far, run)
        forward(far, run, far_over, partner)
        multiply([(far, run)])
        give(far, (6, 4, 5, 7) if run else (2, 3, 0, 1))
    for col in (up_over, down_over):
        for run in range(2):
            arrived(col, run)
            exchange(col, run)
    for col in (up_over, down_over):
        multiply([(col, 0), (col, 1)])
        give(col, all_slots)
    for run in range(2):
        arrived(far_over, run)
        exchange(far_over, run)
    multiply([(far_over, 0), (far_over, 1)])
    give(far_over, all_slots)
    multiply([(up, 0), (up, 1), (down, 0), (down, 1)])
    give(up, all_slots)
    give(down, all_slots)

    own = pltpu.make_async_copy(res.at[0, 0, 7], out_ref.at[home, :], own_sem)
    own.start()
    own.wait()

    def sent(ref, send):
        remote(ref, ref, send, own_sem, sibling).wait_send()

    sent(gath.at[0, 0, :, pl.ds(0, 240), :], z_send)
    sent(gath.at[pl.ds(0, 7), 0], f_send)
    sent(gath.at[:, 0], c_send)
    sent(ener.at[0, 0, pl.ds(0, 56), :], e_send)
    sent(ener.at[pl.ds(0, 7), 0], e_send)
    sent(ener.at[:, 0], e_send)
    sent(out_ref.at[pl.ds(0, 127 * 32), :], r_send)
    take(out_ref.at[pl.ds(0, 127 * 32), :], r_recv)


def shards(amplitudes, integrals, occ_pairs, vir_pairs):
    f32, bf16 = jnp.float32, jnp.bfloat16
    dma = pltpu.SemaphoreType.DMA
    out = pl.pallas_call(
        kernel,
        out_shape=pltpu.VMEM((4096, 128), f32),
        in_specs=[pl.BlockSpec(memory_space=pltpu.HBM)] * 4,
        out_specs=pl.BlockSpec(memory_space=pl.ANY),
        scratch_shapes=[
            pltpu.VMEM((8, 1024), f32),
            pltpu.SMEM((4,), f32),
            pltpu.VMEM((8, 128), f32),
            pltpu.VMEM((64, 128), f32),
            pltpu.VMEM((8, 128), f32),
            pltpu.VMEM((8, 2, 2, 256, 128), f32),
            pltpu.VMEM((8, 2, 64, 128), f32),
            pltpu.VMEM((1024, 2048), f32),
            pltpu.VMEM((2048, 1024), bf16),
            pltpu.VMEM((2048, 1024), bf16),
            pltpu.VMEM((256, 2048), bf16),
            pltpu.VMEM((8, 2, 8, 32, 128), f32),
            dma((3,)), dma((PIECES,)),
            dma, dma((2,)), dma, dma((8, 2)), dma, dma((8, 2)),
            dma, dma((2,)), dma((8, 2)), dma((8, 2)), dma, dma, dma,
        ],
        compiler_params=pltpu.CompilerParams(
            collective_id=0, has_side_effects=True, vmem_limit_bytes=56 << 20
        ),
    )(amplitudes, integrals, occ_pairs, vir_pairs.reshape(8, 128))
    return out.reshape(1024, 4, 128).transpose(1, 0, 2).reshape(4, 131072)


def solution(mesh):
    finer = Mesh(mesh.devices.reshape(8, 4, 2, 2, 2), AXES)
    ab = ("z", "y", "xh", "c")
    in_specs = (P(ab, "xl"), P(ab, None), P(AXES), P(ab))
    return jax.shard_map(
        shards, mesh=finer, in_specs=in_specs, out_specs=P(AXES, None), check_vma=False
    )
```

```python
import jax
import jax.numpy as jnp
from jax import lax
from jax.experimental import pallas as pl
from jax.experimental.pallas import tpu as pltpu
from jax.sharding import Mesh
from jax.sharding import PartitionSpec as P

AXES = ("z", "y", "xh", "c", "xl")
MESH = pl.DeviceIdType.MESH

DIST = (1, 7, 2, 6, 3, 5, 4, 0)
PIECES = 8


def column(dy, dx):
    return dy % 4 + 4 * dx


def split(x):
    hi = x.astype(jnp.bfloat16)
    lo = (x - hi.astype(jnp.float32)).astype(jnp.bfloat16)
    return hi, lo


def kernel(
    amp_hbm, int_hbm, occ_hbm, vir_hbm, out_ref,
    amp, occ_ref, vir_ref, flat, etile, gath, ener, stage, bhi, blo, acat, res,
    in_sem, b_sem, z_send, z_recv, f_send, f_recv, c_send, c_recv,
    e_send, ez_recv, ef_recv, ec_recv, r_send, r_recv, own_sem,
):
    z, y, xh, c, xl = (lax.axis_index(a) for a in AXES)
    block = ((z * 4 + y) * 2 + xh) * 2 + c
    partner = (z, y, 1 - xh, c, 1 - xl)
    sibling = (z, y, xh, 1 - c, xl)

    def along_y(d):
        return (z, lax.rem(y + d, 4), xh, c, xl)

    inputs = [
        pltpu.make_async_copy(amp_hbm, amp, in_sem.at[0]),
        pltpu.make_async_copy(occ_hbm, occ_ref, in_sem.at[1]),
        pltpu.make_async_copy(vir_hbm, vir_ref, in_sem.at[2]),
    ]
    for copy in inputs:
        copy.start()

    def piece(i):
        rows = pl.ds(i * 128, 128)
        return pltpu.make_async_copy(int_hbm.at[rows, :], stage.at[rows, :], b_sem.at[i])

    for i in range(PIECES):
        piece(i).start()

    barrier = pltpu.get_barrier_semaphore()
    peers = [(lax.rem(z + d, 8), y, xh, c, xl) for d in range(1, 8)]
    peers += [(lax.rem(z + d, 8), y, xh, c, 1 - xl) for d in range(8)]
    peers += [along_y(d) for d in range(1, 4)]
    peers += [partner, sibling]
    for peer in peers:
        pl.semaphore_signal(barrier, inc=1, device_id=peer, device_id_type=MESH)

    for copy in inputs:
        copy.wait()
    for s in range(8):
        flat[pl.ds(s, 8, stride=8), :] = amp[:, pl.ds(s * 128, 128)]
    lane_row = lax.broadcasted_iota(jnp.int32, (8, 128), 0)
    energy = jnp.where(lane_row % 4 == 0, occ_ref[0], occ_ref[1])
    energy = jnp.where(lane_row % 4 == 2, occ_ref[2], energy)
    energy = jnp.where(lane_row % 4 == 3, occ_ref[3], energy)
    etile[...] = energy
    ener[0, 0, pl.ds(56, 8), :] = energy
    gath[0, 0, xl, pl.ds(224, 32), :] = flat[pl.ds(pl.multiple_of(xl * 32, 32), 32), :]

    def prepare(i):
        piece(i).wait()

        rows = pl.ds(i * 128, 128)
        hi, lo = split(stage[rows, :].T)
        bhi[:, rows] = hi
        blo[:, rows] = lo

    pl.semaphore_wait(barrier, len(peers))

    def remote(src, dst, send, recv, device):
        return pltpu.make_async_remote_copy(
            src_ref=src, dst_ref=dst, send_sem=send, recv_sem=recv,
            device_id=device, device_id_type=MESH,
        )

    def take(ref, recv):
        remote(ref, ref, own_sem, recv, sibling).wait_recv()

    for k, d in enumerate(DIST):
        zd = lax.rem(z + 8 - d, 8)
        rows = pl.ds(k * 32, 32)
        for j in (xl, 1 - xl) if d else (1 - xl,):
            remote(
                flat.at[pl.ds(pl.multiple_of(j * 32, 32), 32), :],
                gath.at[0, 0, xl, rows, :],
                z_send, z_recv.at[k // 4], (zd, y, xh, c, j),
            ).start()
        if d:
            remote(
                etile, ener.at[0, 0, pl.ds(k * 8, 8), :], e_send, ez_recv.at[k // 4],
                (zd, y, xh, c, xl),
            ).start()

    def part(col, core, run):
        return gath.at[col, core, :, pl.ds(run * 128, 128), :]

    def levels(col, core, run):
        return ener.at[col, core, pl.ds(run * 32, 32), :]

    def forward(col, run, to, device):
        remote(
            part(col, 0, run), part(to, 0, run), f_send, f_recv.at[to, run], device
        ).start()
        remote(
            levels(col, 0, run), levels(to, 0, run), e_send, ef_recv.at[to, run], device
        ).start()

    def arrived(col, run):
        take(part(col, 0, run), f_recv.at[col, run])
        take(levels(col, 0, run), ef_recv.at[col, run])

    def exchange(col, run):
        remote(part(col, 0, run), part(col, 1, run), c_send, c_recv.at[col, run], sibling).start()
        remote(
            levels(col, 0, run), levels(col, 1, run), e_send, ec_recv.at[col, run], sibling
        ).start()

    upper = lax.broadcasted_iota(jnp.int32, (2, 8, 128), 1) < 4
    home = pl.ds(pl.multiple_of(block * 32, 32), 32)

    def multiply(parts, early=()):
        m = 32 * len(parts)
        occ = []
        for i, (col, run) in enumerate(parts):
            take(part(col, 1, run), c_recv.at[col, run])
            take(levels(col, 1, run), ec_recv.at[col, run])
            for core in range(2):
                base = 32 * i + 16 * core
                for h in range(2):
                    for s in range(8):
                        rows = pl.ds(run * 128 + s, 16, stride=8)
                        hi, lo = split(gath[col, core, h, rows, :])
                        lanes = pl.ds((h * 8 + s) * 128, 128)
                        acat[pl.ds(base, 16), lanes] = hi
                        acat[pl.ds(m + base, 16), lanes] = lo
                pairs = ener[col, core, pl.ds(run * 32, 32), :].reshape(2, 2, 8, 128)
                occ.append(jnp.where(upper, pairs[:, 0], pairs[:, 1]))

        for nb in range(4):
            lanes = pl.ds(nb * 256, 256)
            high = jnp.dot(
                acat[pl.ds(0, 2 * m), :], bhi[:, lanes], preferred_element_type=jnp.float32
            )
            low = jnp.dot(
                acat[pl.ds(0, m), :], blo[:, lanes], preferred_element_type=jnp.float32
            )
            total = high[:m] + (high[m:] + low)
            for i, (col, run) in enumerate(parts):
                for core in range(2):
                    base = 32 * i + 16 * core
                    tiles = []
                    for t in range(2):
                        value = total[base : base + 16, 128 * t : 128 * t + 128]
                        vir = vir_ref[pl.ds(nb * 2 + t, 1), :]
                        tiles.append(
                            value.reshape(2, 8, 128) / (vir[None] - occ[2 * i + core])
                        )
                    even = jnp.where(upper, tiles[0], pltpu.roll(tiles[1], 4, 1))
                    odd = jnp.where(upper, pltpu.roll(tiles[0], 4, 1), tiles[1])
                    for b in range(2):
                        k = 4 * run + 2 * b
                        res[col, core, k, pl.ds(nb * 8, 8), :] = even[b]
                        res[col, core, k + 1, pl.ds(nb * 8, 8), :] = odd[b]
            if early and nb % 2:
                give(parts[0][0], early, nb // 2)

    def give(col, slots, half=None):
        cut = pl.ds(0, 32) if half is None else pl.ds(half * 16, 16)
        start = block * 32 if half is None else block * 32 + half * 16
        place = pl.ds(pl.multiple_of(start, 16), 32 if half is None else 16)
        yd = lax.rem(y + col % 4, 4)
        xhd, xld = (1 - xh, 1 - xl) if col >= 4 else (xh, xl)
        for k in slots:
            zd = lax.rem(z + DIST[k], 8)
            for core in range(2):
                if col == 0 and core == 0 and DIST[k] == 0:
                    continue
                cd = 1 - c if core else c
                remote(
                    res.at[col, core, k, cut, :], out_ref.at[place, :], r_send, r_recv,
                    (zd, yd, xhd, cd, xld),
                ).start()

    here, up, far, down = (column(d, 0) for d in range(4))
    over, up_over, far_over, down_over = (column(d, 1) for d in range(4))
    near_slots, far_slots = (2, 3, 0, 1), (6, 4, 5, 7)
    all_slots = (6, 4, 5, 2, 3, 0, 1, 7)

    for i in range(6):
        prepare(i)
    for run in range(2):
        take(gath.at[0, 0, :, pl.ds(0, 112 if run else 128), :], z_recv.at[run])
        take(ener.at[0, 0, pl.ds(0, 24 if run else 32), :], ez_recv.at[run])
        exchange(here, run)
        forward(here, run, over, partner)
        forward(here, run, down, along_y(1))
        forward(here, run, up, along_y(3))
        if run == 0:
            for i in range(6, 8):
                prepare(i)
        multiply([(here, run)], (6, 4, 5, 7) if run else (2, 3, 0, 1))
    for run in range(2):
        arrived(over, run)
        exchange(over, run)
        for col in (up, down):
            arrived(col, run)
            exchange(col, run)
        if run == 0:
            forward(down, 0, far, along_y(1))
        else:
            forward(up, 1, far, along_y(3))
        forward(over, run, down_over, along_y(1))
        forward(over, run, up_over, along_y(3))
        multiply([(over, run)])
        give(over, (6, 4, 5, 7) if run else (2, 3, 0, 1))
    for run in range(2):
        arrived(far, run)
        exchange(far, run)
        forward(far, run, far_over, partner)
        multiply([(far, run)])
        give(far, (6, 4, 5, 7) if run else (2, 3, 0, 1))
    for col in (up_over, down_over):
        for run in range(2):
            arrived(col, run)
            exchange(col, run)
    for col in (up_over, down_over):
        multiply([(col, 0), (col, 1)])
        give(col, all_slots)
    for run in range(2):
        arrived(far_over, run)
        exchange(far_over, run)
    multiply([(far_over, 0), (far_over, 1)])
    give(far_over, all_slots)
    multiply([(up, 0), (up, 1), (down, 0), (down, 1)])
    give(up, all_slots)
    give(down, all_slots)

    own = pltpu.make_async_copy(res.at[0, 0, 7], out_ref.at[home, :], own_sem)
    own.start()
    own.wait()

    def sent(ref, send):
        remote(ref, ref, send, own_sem, sibling).wait_send()

    sent(gath.at[0, 0, :, pl.ds(0, 240), :], z_send)
    sent(gath.at[pl.ds(0, 7), 0], f_send)
    sent(gath.at[:, 0], c_send)
    sent(ener.at[0, 0, pl.ds(0, 56), :], e_send)
    sent(ener.at[pl.ds(0, 7), 0], e_send)
    sent(ener.at[:, 0], e_send)
    sent(out_ref.at[pl.ds(0, 127 * 32), :], r_send)
    take(out_ref.at[pl.ds(0, 127 * 32), :], r_recv)


def shards(amplitudes, integrals, occ_pairs, vir_pairs):
    f32, bf16 = jnp.float32, jnp.bfloat16
    dma = pltpu.SemaphoreType.DMA
    out = pl.pallas_call(
        kernel,
        out_shape=pltpu.VMEM((4096, 128), f32),
        in_specs=[pl.BlockSpec(memory_space=pltpu.HBM)] * 4,
        out_specs=pl.BlockSpec(memory_space=pl.ANY),
        scratch_shapes=[
            pltpu.VMEM((8, 1024), f32),
            pltpu.SMEM((4,), f32),
            pltpu.VMEM((8, 128), f32),
            pltpu.VMEM((64, 128), f32),
            pltpu.VMEM((8, 128), f32),
            pltpu.VMEM((8, 2, 2, 256, 128), f32),
            pltpu.VMEM((8, 2, 64, 128), f32),
            pltpu.VMEM((1024, 2048), f32),
            pltpu.VMEM((2048, 1024), bf16),
            pltpu.VMEM((2048, 1024), bf16),
            pltpu.VMEM((256, 2048), bf16),
            pltpu.VMEM((8, 2, 8, 32, 128), f32),
            dma((3,)), dma((PIECES,)),
            dma, dma((2,)), dma, dma((8, 2)), dma, dma((8, 2)),
            dma, dma((2,)), dma((8, 2)), dma((8, 2)), dma, dma, dma,
        ],
        compiler_params=pltpu.CompilerParams(
            collective_id=0, has_side_effects=True, vmem_limit_bytes=56 << 20
        ),
    )(amplitudes, integrals, occ_pairs, vir_pairs.reshape(8, 128))
    return out.reshape(1024, 4, 128).transpose(1, 0, 2).reshape(4, 131072)


def solution(mesh):
    finer = Mesh(mesh.devices.reshape(8, 4, 2, 2, 2), AXES)
    ab = ("z", "y", "xh", "c")
    in_specs = (P(ab, "xl"), P(ab, None), P(AXES), P(ab))
    return jax.shard_map(
        shards, mesh=finer, in_specs=in_specs, out_specs=P(AXES, None), check_vma=False
    )
```
